32 devices in a mesh: gx: 4 (over y, core), yz: 8 (over z, x).
Axes of the slice: x: 2, y: 2, z: 4, core: 2. Of those that a mesh axis runs over, the one named last changes fastest.
Arguments:
- flow_speed_field: float32 [3, 32, 64, 128], P(None, 'gx', 'yz'), may hold values from -6 to 6
- thermal_field: float32 [32, 64, 128], P('gx', 'yz'), may hold values from 0.5 to 2
- walker_speed_vectors: float32 [3, 4096, 128], P(None, ('gx', 'yz')), may hold values from -6 to 6
- walker_statistical_mass: float32 [4096, 128], P(('gx', 'yz')), may hold values from 0.5 to 2
- gaussian_samples: float32 [2, 3, 4096, 128], P(None, None, ('gx', 'yz')), may hold values from -6 to 6
- walker_strip_position: int32 [4096, 128], P(('gx', 'yz')), may hold values from 0 to 127
- group_active_tally: int32 [4096], P(('gx', 'yz')), may hold values from 32 to 128
- group_resident_strip: int32 [4096], P(('gx', 'yz')), may hold values from 0 to 63
- migrating_group_table: int32 [512], P(('gx', 'yz')), may hold values from 0 to 127, as said below
- target_processor_slot: int32 [512, 1], P(('gx', 'yz')), may hold values from 0 to 7; in each aligned block of 16 rows (0 to 15, 16 to 31, ...) at most 4 rows name the same one
- entered_strip_slot: int32 [512], P(('gx', 'yz')), may hold values from 0 to 63
Outputs:
- new_fields: float32 [4, 32, 64, 128], P(None, 'gx', 'yz')
- particle_velocity: float32 [3, 4096, 128], P(None, ('gx', 'yz'))
The draws below stay inside these ranges and needn't reach their ends.
Inputs may be any that keep to these rules, and one draw needn't show every extreme that they name: `migrating_group_table`: within each device's 16 entries the block indices are distinct. `target_processor_slot`: among the 16 rows of one device no yz index appears more than 4 times.
All inputs are finite; a program needn't handle non-finite values.
Results may differ from the reference program's by a relative error of at most 0.00005.
Values sent between devices are 32-bit elements; how exact they have to be, the bound alone decides.
A program may use at most 64 MiB of HBM per device.

```python
import math
import jax
import jax.numpy as jnp
import numpy as np
from jax import lax

CX = 8
CY = 8
CZ = 128
SLOTS = 128
BLK_DEV = 128
MIG_DEV = 16
CAP = 4
PENCILS = 64
GRID_SPAN_X = 32
GRID_SPAN_Y = 64
GRID_SPAN_Z = 128
NBLK = 4096
MIGS = 512
N_GX = 4
N_YZ = 8


def draw_migrating_group_table(key, part):
    keys = jax.random.split(key, N_GX * N_YZ)

    def pick(single):
        return jax.random.permutation(single, BLK_DEV)[:MIG_DEV].astype(jnp.int32)
    return jax.vmap(pick)(keys).reshape(-1)


def touch_ends(entries, stream_key, low, largest):
    extent = entries.shape
    spot = [jax.random.randint(jax.random.fold_in(stream_key, axis), (), 0, extent[axis]) for axis in range(len(extent))]
    entries = entries.at[tuple(spot)].set(low)
    longest = extent.index(max(extent))
    spot[longest] = (spot[longest] + 1) % extent[longest]
    return entries.at[tuple(spot)].set(largest)


def block_levels(stream_key, shape, shards, low, largest):
    level = 1.0
    for dim, shards_of in shards:
        heights = jax.random.uniform(jax.random.fold_in(jax.random.fold_in(stream_key, 6), dim), (shards_of,), jnp.float32, low / len(shards), largest / len(shards))
        level = level * jnp.repeat(jnp.exp(heights), shape[dim] // shards_of).reshape((-1,) + (1,) * (len(shape) - 1 - dim))
    return level


def deal_out(stream_key, own, number, rows, amount, top, limit, lean):
    sequence = jax.random.permutation(stream_key, amount)
    packed, ordinary = load_shares(amount, rows * top, limit, lean, True), load_shares(amount, rows * top, limit, lean, False)
    places = jnp.arange(amount)

    def named(sizes, offset_by):
        used = int((sizes > 0).sum())
        fixed = max(1, used // 4)
        shifted = fixed + (places - fixed + offset_by * (used - fixed)) % max(1, amount - fixed)
        return jnp.zeros((amount,), jnp.int32).at[sequence[jnp.where(places < fixed, places, shifted)]].set(jnp.asarray(sizes, jnp.int32))

    sizes = jnp.where(number % 4 == 0, named(packed, number // 4), named(ordinary, number - number // 4 - 1))
    mixed = jax.random.permutation(jax.random.fold_in(own, 3), amount)
    giver, sink = mixed[0:amount // 2 * 2:2], mixed[1:amount // 2 * 2:2]
    slack = jnp.minimum(sizes[giver] - 1, limit - sizes[sink]) // 2
    slack = jnp.where((giver == sequence[0]) | (sink == sequence[0]) | (sizes[sink] == 0), 0, jnp.maximum(slack, 0))
    shifted = jax.random.randint(jax.random.fold_in(own, 4), (amount // 2,), 0, 1 << 20) % (slack + 1)
    sizes = sizes.at[giver].add(-shifted).at[sink].add(shifted)
    items = jnp.searchsorted(jnp.cumsum(sizes), jnp.arange(rows * top), side="right").astype(jnp.int32)
    grid = items.reshape(top, rows).T
    grid = grid[jax.random.permutation(jax.random.fold_in(own, 1), rows)]
    offset_by = jax.random.randint(jax.random.fold_in(own, 2), (rows, 1), 0, top)
    return jnp.take_along_axis(grid, (jnp.arange(top)[None, :] + offset_by) % top, axis=1)


def load_shares(number_of, total, limit, skew, full):
    loads = [(1 << 20) // math.isqrt(grade ** skew) + 1 for grade in range(1, number_of + 1)]
    largest = limit if full else min(limit, max(-(-total // number_of), total * loads[0] // sum(loads)))
    least = 1 if total - largest >= number_of - 1 else 0
    holding, surplus = [largest] + [least] * (number_of - 1), total - largest - least * (number_of - 1)
    while surplus > 0:
        movable = [i for i in range(1, number_of) if holding[i] < largest] or [i for i in range(1, number_of) if holding[i] < limit]
        pool, left = sum([loads[i] for i in movable]), surplus
        for i in movable:
            more = min(limit - holding[i], max(1, left * loads[i] // pool), surplus)
            holding[i] = holding[i] + more
            surplus = surplus - more
    return np.array(holding)


def centred(own_key, dims, spread, bound, cuts=(), kind=jnp.bfloat16):
    entries = spread * jax.random.normal(own_key, dims, jnp.float32)
    if cuts:
        entries = entries * block_levels(own_key, dims, cuts, -0.22, 0.18)
    return jnp.clip(entries, -bound, bound).astype(kind)


def setup_inputs(seed: int = 0) -> dict:
    arg_keys = jax.random.split(jax.random.key(seed), 12)
    flow_speed_field = centred(arg_keys[0], (3, GRID_SPAN_X, GRID_SPAN_Y, GRID_SPAN_Z), 1.0, 6.0, ((1, 4), (2, 8)), jnp.float32)
    thermal_field = jnp.clip(jnp.exp(math.log(2.0) - 1.3862944 * jax.random.uniform(arg_keys[1], (GRID_SPAN_X, GRID_SPAN_Y, GRID_SPAN_Z), jnp.float32) ** block_levels(arg_keys[1], (GRID_SPAN_X, GRID_SPAN_Y, GRID_SPAN_Z), ((0, 4), (1, 8)), -0.2, 0.2)), 0.5, 2.0)
    walker_speed_vectors = centred(arg_keys[2], (3, NBLK, SLOTS), 1.0, 6.0, ((1, 32),), jnp.float32)
    walker_statistical_mass = jnp.clip(jnp.exp(math.log(2.0) - 1.3862944 * jax.random.uniform(arg_keys[3], (NBLK, SLOTS), jnp.float32) ** block_levels(arg_keys[3], (NBLK, SLOTS), ((0, 32),), -0.2, 0.2)), 0.5, 2.0)
    gaussian_samples = centred(arg_keys[4], (2, 3, NBLK, SLOTS), 1.0, 6.0, ((2, 32),), jnp.float32)
    walker_strip_position = touch_ends(jax.random.randint(arg_keys[5], (NBLK, SLOTS), 0, CZ), jax.random.fold_in(arg_keys[5], 1), 0, CZ - 1).astype(jnp.int32)
    group_active_tally = touch_ends(jax.random.randint(arg_keys[6], (NBLK,), SLOTS // 4, SLOTS + 1), jax.random.fold_in(arg_keys[6], 1), SLOTS // 4, SLOTS).astype(jnp.int32)
    group_resident_strip = touch_ends(jax.random.randint(arg_keys[7], (NBLK,), 0, PENCILS), jax.random.fold_in(arg_keys[7], 1), 0, PENCILS - 1).astype(jnp.int32)
    migrating_group_table = draw_migrating_group_table(jax.random.fold_in(arg_keys[11], 71), 0)
    target_processor_slot_keys = jax.random.split(jax.random.fold_in(arg_keys[9], 1), MIGS // MIG_DEV)
    target_processor_slot_turns = jax.random.permutation(jax.random.fold_in(arg_keys[9], 3), MIGS // MIG_DEV)
    target_processor_slot = jax.vmap(lambda own, number: deal_out(jax.random.fold_in(arg_keys[9], 2), own, number, MIG_DEV, N_YZ, 1, CAP, 2))(target_processor_slot_keys, target_processor_slot_turns).reshape((MIGS, 1))
    entered_strip_slot = touch_ends(jax.random.randint(arg_keys[10], (MIGS,), 0, PENCILS), jax.random.fold_in(arg_keys[10], 1), 0, PENCILS - 1).astype(jnp.int32)
    return dict(flow_speed_field=flow_speed_field, thermal_field=thermal_field, walker_speed_vectors=walker_speed_vectors, walker_statistical_mass=walker_statistical_mass, gaussian_samples=gaussian_samples, walker_strip_position=walker_strip_position, group_active_tally=group_active_tally, group_resident_strip=group_resident_strip, migrating_group_table=migrating_group_table, target_processor_slot=target_processor_slot, entered_strip_slot=entered_strip_slot)


DECAY = 0.6
VISCOSITY = 0.05
COUPLING = 0.02
STRESS_GAIN = 0.005
RELAXATION = 0.5
PAIRS = ((0, 0), (0, 1), (0, 2), (1, 1), (1, 2), (2, 2))
PAIR_INDEX = ((0, 1, 2), (1, 3, 4), (2, 4, 5))

def neighbour(padded, axis, offset):
    sizes = [padded.shape[1] - 2, padded.shape[2] - 2, padded.shape[3] - 2]
    begin = [1, 1, 1]
    begin[axis] = 1 + offset
    return padded[:, begin[0]:begin[0] + sizes[0], begin[1]:begin[1] + sizes[1], begin[2]:begin[2] + sizes[2]]

def laplace(padded):
    total = neighbour(padded, 0, 1) + neighbour(padded, 0, -1)
    total = total + neighbour(padded, 1, 1) + neighbour(padded, 1, -1)
    total = total + neighbour(padded, 2, 1) + neighbour(padded, 2, -1)
    return total - 6.0 * neighbour(padded, 0, 0)

def fluid_step(padded_fields, padded_stress, moments):
    flow = neighbour(padded_fields, 0, 0)[:3]
    heat = neighbour(padded_fields, 0, 0)[3]
    density = moments[0]
    momentum = moments[1:4]
    stress = moments[4:10]
    smooth = laplace(padded_fields)
    slopes = [0.5 * (neighbour(padded_stress, axis, 1) - neighbour(padded_stress, axis, -1)) for axis in range(3)]
    divergence = jnp.stack([slopes[0][PAIR_INDEX[row][0]] + slopes[1][PAIR_INDEX[row][1]] + slopes[2][PAIR_INDEX[row][2]] for row in range(3)])
    new_flow = flow + VISCOSITY * smooth[:3] + COUPLING * (momentum - density[None] * flow) - STRESS_GAIN * divergence
    energy = (stress[0] + stress[3] + stress[5] - 2.0 * lax.optimization_barrier(jnp.sum(momentum * flow, axis=0)) + density * lax.optimization_barrier(jnp.sum(flow * flow, axis=0))) / 3.0
    new_heat = heat + VISCOSITY * smooth[3] + COUPLING * (energy - density * heat)
    return jnp.concatenate([new_flow, new_heat[None]], 0)

def drift_step(start, sampled, noise):
    return sampled[:3] + DECAY * (start - sampled[:3]) + jnp.sqrt((1.0 - DECAY * DECAY) * sampled[3])[None] * noise

def sample(mesh_element_measure, column_x, column_y, cells):
    return jnp.take_along_axis(mesh_element_measure[:, column_x, column_y, :], cells[None], axis=2)

def reference(flow_speed_field, thermal_field, walker_speed_vectors, walker_statistical_mass, gaussian_samples, walker_strip_position, group_active_tally, group_resident_strip, migrating_group_table, target_processor_slot, entered_strip_slot):
    blocks = jnp.arange(NBLK, dtype=jnp.int32)
    device = blocks // BLK_DEV
    home_x = device // N_YZ * CX + group_resident_strip // CY
    home_y = device % N_YZ * CY + group_resident_strip % CY
    mover = jnp.arange(MIGS, dtype=jnp.int32) // MIG_DEV
    moved = mover * BLK_DEV + migrating_group_table
    current_x = home_x.at[moved].set(mover // N_YZ * CX + entered_strip_slot // CY)
    current_y = home_y.at[moved].set(target_processor_slot[:, 0] * CY + entered_strip_slot % CY)
    live = (jnp.arange(SLOTS, dtype=jnp.int32)[None, :] < group_active_tally[:, None]).astype(jnp.float32)
    mesh_element_measure = jnp.concatenate([flow_speed_field, thermal_field[None]], 0)
    first = drift_step(walker_speed_vectors, sample(mesh_element_measure, home_x, home_y, walker_strip_position), gaussian_samples[0])
    second = drift_step(first, sample(mesh_element_measure, current_x, current_y, walker_strip_position), gaussian_samples[1])
    weight = walker_statistical_mass * live
    flat = ((current_x[:, None] * GRID_SPAN_Y + current_y[:, None]) * GRID_SPAN_Z + walker_strip_position).reshape(-1)
    terms = [weight] + [weight * second[row] for row in range(3)] + [weight * second[one] * second[two] for one, two in PAIRS]
    moments = jnp.stack([jax.ops.segment_sum(term.reshape(-1), flat, num_segments=GRID_SPAN_X * GRID_SPAN_Y * GRID_SPAN_Z) for term in terms]).reshape(10, GRID_SPAN_X, GRID_SPAN_Y, GRID_SPAN_Z)
    widths = ((0, 0), (1, 1), (1, 1), (1, 1))
    new_cube = fluid_step(jnp.pad(mesh_element_measure, widths), jnp.pad(moments[4:10], widths), moments)
    after = sample(new_cube, current_x, current_y, walker_strip_position)
    final = second + RELAXATION * (after[:3] - second)
    return (new_cube, final * live[None])
```

```python
import functools

import jax
import jax.numpy as jnp
from jax import lax
from jax.experimental import pallas as pl
from jax.experimental.pallas import tpu as pltpu
from jax.sharding import PartitionSpec as P

DECAY = 0.6
VISCOSITY = 0.05
COUPLING = 0.02
STRESS_GAIN = 0.005
RELAXATION = 0.5
PAIRS = ((0, 0), (0, 1), (0, 2), (1, 1), (1, 2), (2, 2))
PAIR_INDEX = ((0, 1, 2), (1, 3, 4), (2, 4, 5))
MOMENTS = 10
PITCH = 16
SENT = 9
MESH = pl.DeviceIdType.MESH
BF16 = jnp.bfloat16
F32 = jnp.float32


def split3(x):
    high = x.astype(BF16)
    rest = x - high.astype(F32)
    mid = rest.astype(BF16)
    low = (rest - mid.astype(F32)).astype(BF16)
    return high, mid, low


def dot(a, b):
    return jnp.dot(a, b, preferred_element_type=F32)


def dot_last(a, b):
    return lax.dot_general(a, b, (((1,), (1,)), ((), ())), preferred_element_type=F32)


def pick(onehot, x):
    high, mid, low = split3(x)
    return dot(onehot, high) + dot(onehot, mid) + dot(onehot, low)


def lanes(x, index):
    return jnp.take_along_axis(x, index, axis=1, mode="promise_in_bounds")


def onehot(condition):
    return jnp.where(condition, 1.0, 0.0)


def drift(start, u, spread, noise):
    return u + DECAY * (start - u) + spread * noise


def deposit(count, unroll, v_ref, cells_ref, pb_ref):
    width = v_ref.shape[1]
    slots = cells_ref.shape[1]
    where = lax.broadcasted_iota(jnp.int32, (width, slots), 0)

    def some(step, carry):
        for t in range(unroll):
            n = step * unroll + t
            row = pl.ds(pl.multiple_of(n * PITCH, PITCH), PITCH)
            lhs = jnp.concatenate(split3(v_ref[row, :]), axis=0)
            hot = onehot(cells_ref[pl.ds(n, 1), :] == where).astype(BF16)
            out = dot_last(lhs, hot)
            pb_ref[row, :] = out[:PITCH] + out[PITCH : 2 * PITCH] + out[2 * PITCH :]
        return carry

    lax.fori_loop(0, count // unroll, some, 0)


def put_terms(v_ref, count, weight, second):
    terms = (
        [weight]
        + [weight * second[row] for row in range(3)]
        + [weight * second[one] * second[two] for one, two in PAIRS]
    )
    for k, term in enumerate(terms):
        v_ref[pl.ds(k, count, stride=PITCH), :] = term


def kernel(
    n,
    n_gx,
    spans,
    flow,
    heat,
    speed,
    mass,
    noise,
    cells,
    tally,
    home,
    table,
    target,
    entered,
    fields_out,
    speed_out,
    v_ref,
    pb_ref,
    second_ref,
    cells_a,
    moments,
    wide,
    face_send,
    face_recv,
    stress_send,
    stress_recv,
    out_ref,
    in_ref,
    back_send,
    back_recv,
    out_s,
    out_r,
    face_s,
    face_r,
    stress_s,
    stress_r,
    back_s,
    back_r,
):
    X, Y, Z = spans
    pencils = X * Y
    blocks, slots = mass.shape
    moving = table.shape[1]
    cap = 2 * moving // n
    received = n * cap
    rows = out_ref.shape[0] // n
    back_rows = back_send.shape[0] // n
    gx = lax.axis_index("gx")
    me = lax.axis_index("yz")
    peers = [(i, lax.rem(me + i, n), lax.rem(me + n - i, n)) for i in range(1, n)]

    barrier = pltpu.get_barrier_semaphore()
    for _, peer, _ in peers:
        pl.semaphore_signal(barrier, inc=1, device_id={"yz": peer}, device_id_type=MESH)

    @pl.when(gx > 0)
    def _():
        pl.semaphore_signal(barrier, inc=1, device_id={"gx": gx - 1}, device_id_type=MESH)

    @pl.when(gx < n_gx - 1)
    def _():
        pl.semaphore_signal(barrier, inc=1, device_id={"gx": gx + 1}, device_id_type=MESH)

    sides = (
        (0, 1, gx > 0, gx == 0, {"gx": gx - 1}),
        (1, 0, gx < n_gx - 1, gx == n_gx - 1, {"gx": gx + 1}),
        (2, 3, me > 0, me == 0, {"yz": me - 1}),
        (3, 2, me < n - 1, me == n - 1, {"yz": me + 1}),
    )
    for side, _, _, edge, _ in sides:

        @pl.when(edge)
        def _(side=side):
            face_recv[side] = jnp.zeros(face_recv.shape[1:], F32)
            stress_recv[side] = jnp.zeros(stress_recv.shape[1:], F32)

    def face_copy(side, other, where, send, recv, send_sem, recv_sem):
        return pltpu.make_async_remote_copy(
            src_ref=send.at[side],
            dst_ref=recv.at[other],
            send_sem=send_sem.at[side],
            recv_sem=recv_sem.at[other],
            device_id=where,
            device_id_type=MESH,
        )

    def faces_start(send, recv, send_sem, recv_sem):
        for side, other, there, _, where in sides:

            @pl.when(there)
            def _(side=side, other=other, where=where):
                face_copy(side, other, where, send, recv, send_sem, recv_sem).start()

    def faces_wait(send, recv, send_sem, recv_sem):
        for side, _, there, _, where in sides:

            @pl.when(there)
            def _(side=side, where=where):
                face_copy(side, side, where, send, recv, send_sem, recv_sem).wait_recv()

    def faces_sent(send, recv, send_sem, recv_sem):
        for side, other, there, _, where in sides:

            @pl.when(there)
            def _(side=side, other=other, where=where):
                face_copy(side, other, where, send, recv, send_sem, recv_sem).wait_send()

    face_args = (face_send, face_recv, face_s, face_r)
    stress_args = (stress_send, stress_recv, stress_s, stress_r)

    def all_copy(i, peer, send, recv, height, send_sem, recv_sem):
        return pltpu.make_async_remote_copy(
            src_ref=send.at[pl.ds(pl.multiple_of(peer * height, 8), height), :],
            dst_ref=recv.at[pl.ds(pl.multiple_of(me * height, 8), height), :],
            send_sem=send_sem.at[i],
            recv_sem=recv_sem.at[i],
            device_id={"yz": peer},
            device_id_type=MESH,
        )

    def all_start(send, recv, height, send_sem, recv_sem):
        for i, peer, _ in peers:
            all_copy(i, peer, send, recv, height, send_sem, recv_sem).start()

    def all_wait(send, recv, height, send_sem, recv_sem):
        for i, _, source in peers:
            pltpu.make_async_remote_copy(
                src_ref=send.at[pl.ds(pl.multiple_of(source * height, 8), height), :],
                dst_ref=recv.at[pl.ds(pl.multiple_of(source * height, 8), height), :],
                send_sem=send_sem.at[i],
                recv_sem=recv_sem.at[i],
                device_id={"yz": source},
                device_id_type=MESH,
            ).wait_recv()

    def all_sent(send, recv, height, send_sem, recv_sem):
        for i, peer, _ in peers:
            all_copy(i, peer, send, recv, height, send_sem, recv_sem).wait_send()

    pay_args = (out_ref, in_ref, rows, out_s, out_r)
    back_args = (back_send, back_recv, back_rows, back_s, back_r)

    for c in range(4):
        grid = flow.at[c] if c < 3 else heat
        face_send[0, c] = grid[pl.ds(0, Y), :]
        face_send[1, c] = grid[pl.ds((X - 1) * Y, Y), :]
        face_send[2, c] = grid[pl.ds(0, X, stride=Y), :]
        face_send[3, c] = grid[pl.ds(Y - 1, X, stride=Y), :]

    iota = functools.partial(lax.broadcasted_iota, jnp.int32)
    eye = iota((moving, moving), 0) == iota((moving, moving), 1)
    target_row = target[...]
    target_col = jnp.sum(jnp.where(eye, target_row, 0), axis=1, keepdims=True)
    earlier = (target_col == target_row) & (iota((moving, moving), 0) < iota((moving, moving), 1))
    rank = jnp.sum(jnp.where(earlier, 1, 0), axis=0, keepdims=True)
    slot_row = rank * n + target_row
    slot_hot = onehot(iota((received, moving), 0) == slot_row)
    block_hot = onehot(iota((blocks, moving), 0) == table[...])
    from_block = dot_last(slot_hot.astype(BF16), block_hot.astype(BF16)).astype(BF16)
    to_block = dot_last(block_hot.astype(BF16), slot_hot.astype(BF16))
    moved = jnp.sum(to_block, axis=1, keepdims=True) > 0.5
    to_block = to_block.astype(BF16)
    pencil_out = jnp.sum(slot_hot * entered[...].astype(F32), axis=1, keepdims=True)

    home_t = onehot(iota((pencils, blocks), 0) == home[...])
    home_hot = home_t.T.astype(BF16)
    home_t = home_t.astype(BF16)
    live = onehot(iota((slots, blocks), 0) < tally[...]).T

    where = cells[...]
    u = [lanes(pick(home_hot, flow[c]), where) for c in range(3)]
    temp = lanes(pick(home_hot, heat[...]), where)
    spread = jnp.sqrt((1.0 - DECAY * DECAY) * temp)
    weight = mass[...] * live
    first = [drift(speed[c], u[c], spread, noise[c]) for c in range(3)]
    sent = [pick(from_block, first[c]) for c in range(3)]
    sent.append(pick(from_block, weight))
    sent += [pick(from_block, noise[3 + c]) for c in range(3)]
    sent.append(dot(from_block, where.astype(F32).astype(BF16)))
    sent.append(jnp.broadcast_to(pencil_out, (received, slots)))
    for c in range(SENT):
        for j in range(cap):
            out_ref[pl.ds(c * cap + j, n, stride=rows), :] = sent[c][j * n : (j + 1) * n]

    expected = n - 1 + jnp.where(gx > 0, 1, 0) + jnp.where(gx < n_gx - 1, 1, 0)
    pl.semaphore_wait(barrier, expected)
    all_start(*pay_args)
    faces_start(*face_args)
    own = pl.ds(pl.multiple_of(me * rows, 8), rows)
    in_ref[own, :] = out_ref[own, :]

    second = [drift(first[c], u[c], spread, noise[3 + c]) for c in range(3)]
    for c in range(3):
        second_ref[c] = second[c]
    put_terms(v_ref, blocks, jnp.where(moved, 0.0, weight), second)
    deposit(blocks, 8, v_ref, cells, pb_ref)
    for k in range(MOMENTS):
        moments[k] = pick(home_t, pb_ref[pl.ds(k, blocks, stride=PITCH), :])

    all_wait(*pay_args)
    got = [
        jnp.concatenate(
            [in_ref[pl.ds(c * cap + j, n, stride=rows), :] for j in range(cap)], axis=0
        )
        for c in range(SENT)
    ]
    where_a = got[7].astype(jnp.int32)
    cells_a[...] = where_a
    pencil_hot = onehot(got[8][:, :pencils].astype(jnp.int32) == iota((received, pencils), 1))
    pencil_t = pencil_hot.T.astype(BF16)
    pencil_hot = pencil_hot.astype(BF16)
    u_a = [lanes(pick(pencil_hot, flow[c]), where_a) for c in range(3)]
    temp_a = lanes(pick(pencil_hot, heat[...]), where_a)
    spread_a = jnp.sqrt((1.0 - DECAY * DECAY) * temp_a)
    second_a = [drift(got[c], u_a[c], spread_a, got[4 + c]) for c in range(3)]
    put_terms(v_ref, received, got[3], second_a)
    deposit(received, 8, v_ref, cells_a, pb_ref)
    for k in range(MOMENTS - 1, -1, -1):
        total = moments[k] + pick(pencil_t, pb_ref[pl.ds(k, received, stride=PITCH), :])
        moments[k] = total
        if k >= 4:
            s = k - 4
            stress_send[0, s] = total[:Y]
            stress_send[1, s] = total[pencils - Y :]
            stress_send[2, s] = moments[k, pl.ds(0, X, stride=Y), :]
            stress_send[3, s] = moments[k, pl.ds(Y - 1, X, stride=Y), :]
    faces_start(*stress_args)

    lane = iota((pencils, Z), 1)

    def along_z(x, step):
        if step > 0:
            return jnp.where(lane == Z - 1, 0.0, pltpu.roll(x, Z - 1, 1))
        return jnp.where(lane == 0, 0.0, pltpu.roll(x, 1, 1))

    def fill(slot, value, halo, c):
        wide[slot, 1 : X + 1, 8 : 8 + Y, :] = value.reshape(X, Y, Z)
        wide[slot, 0, 8 : 8 + Y, :] = halo[0, c]
        wide[slot, X + 1, 8 : 8 + Y, :] = halo[1, c]
        for x in range(X):
            wide[slot, x + 1, 7:8, :] = halo[2, c, x : x + 1]
            wide[slot, x + 1, 8 + Y : 9 + Y, :] = halo[3, c, x : x + 1]

    def along_x(slot, step):
        return wide[slot, 1 + step : 1 + step + X, 8 : 8 + Y, :].reshape(pencils, Z)

    def along_y(slot, step):
        return wide[slot, 1 : X + 1, 8 + step : 8 + step + Y, :].reshape(pencils, Z)

    faces_wait(*face_args)
    f = [flow[0], flow[1], flow[2], heat[...]]
    base = []
    for c in range(4):
        fill(c, f[c], face_recv, c)
        smooth = along_x(c, 1) + along_x(c, -1) + along_y(c, 1) + along_y(c, -1)
        smooth = smooth + along_z(f[c], 1) + along_z(f[c], -1) - 6.0 * f[c]
        base.append(f[c] + VISCOSITY * smooth)
    density = moments[0]
    momentum = [moments[1 + c] for c in range(3)]
    for c in range(3):
        base[c] = base[c] + COUPLING * (momentum[c] - density * f[c])
    dots = momentum[0] * f[0] + momentum[1] * f[1] + momentum[2] * f[2]
    squares = f[0] * f[0] + f[1] * f[1] + f[2] * f[2]
    energy = (moments[4] + moments[7] + moments[9] - 2.0 * dots + density * squares) / 3.0
    fields_out[3] = base[3] + COUPLING * (energy - density * f[3])
    stress = [moments[4 + s] for s in range(6)]
    slope_z = [along_z(stress[s], 1) - along_z(stress[s], -1) for s in (2, 4, 5)]

    faces_wait(*stress_args)
    for s in range(6):
        if s < 5:
            fill(4 + s, stress[s], stress_recv, s)
    fresh = []
    for row in range(3):
        sx, sy, _ = PAIR_INDEX[row]
        slope = along_x(4 + sx, 1) - along_x(4 + sx, -1) + slope_z[row]
        slope = slope + along_y(4 + sy, 1) - along_y(4 + sy, -1)
        value = base[row] - (0.5 * STRESS_GAIN) * slope
        fields_out[row] = value
        fresh.append(split3(value))

    def sampled(hot, c):
        return dot(hot, fresh[c][0]) + dot(hot, fresh[c][1]) + dot(hot, fresh[c][2])

    for c in range(3):
        w = lanes(sampled(pencil_hot, c), where_a)
        third = second_a[c] + RELAXATION * (w - second_a[c])
        for j in range(cap):
            back_send[pl.ds(c * cap + j, n, stride=back_rows), :] = third[j * n : (j + 1) * n]
    all_start(*back_args)
    own = pl.ds(pl.multiple_of(me * back_rows, 8), back_rows)
    back_recv[own, :] = back_send[own, :]
    for c in range(3):
        w = lanes(sampled(home_hot, c), where)
        now = second_ref[c]
        second_ref[c] = live * (now + RELAXATION * (w - now))
    all_wait(*back_args)
    for c in range(3):
        returned = jnp.concatenate(
            [back_recv[pl.ds(c * cap + j, n, stride=back_rows), :] for j in range(cap)], axis=0
        )
        speed_out[c] = jnp.where(moved, live * pick(to_block, returned), second_ref[c])

    all_sent(*pay_args)
    faces_sent(*face_args)
    faces_sent(*stress_args)
    all_sent(*back_args)


def shards(
    flow_speed_field,
    thermal_field,
    walker_speed_vectors,
    walker_statistical_mass,
    gaussian_samples,
    walker_strip_position,
    group_active_tally,
    group_resident_strip,
    migrating_group_table,
    target_processor_slot,
    entered_strip_slot,
):
    n = lax.axis_size("yz")
    n_gx = lax.axis_size("gx")
    X, Y, Z = thermal_field.shape
    blocks, slots = walker_statistical_mass.shape
    moving = migrating_group_table.shape[0]
    cap = 2 * moving // n
    received = n * cap
    rows = -(-SENT * cap // 8) * 8
    back_rows = -(-3 * cap // 8) * 8
    vmem = pl.BlockSpec(memory_space=pltpu.VMEM)
    fields, velocity = pl.pallas_call(
        functools.partial(kernel, n, n_gx, (X, Y, Z)),
        out_shape=(
            jax.ShapeDtypeStruct((4, X * Y, Z), F32),
            jax.ShapeDtypeStruct((3, blocks, slots), F32),
        ),
        in_specs=[vmem] * 11,
        out_specs=(vmem, vmem),
        scratch_shapes=[
            pltpu.VMEM((max(blocks, received) * PITCH, slots), F32),
            pltpu.VMEM((max(blocks, received) * PITCH, Z), F32),
            pltpu.VMEM((3, blocks, slots), F32),
            pltpu.VMEM((received, slots), jnp.int32),
            pltpu.VMEM((MOMENTS, X * Y, Z), F32),
            pltpu.VMEM((9, X + 2, 24, Z), F32),
            pltpu.VMEM((4, 4, 8, Z), F32),
            pltpu.VMEM((4, 4, 8, Z), F32),
            pltpu.VMEM((4, 6, 8, Z), F32),
            pltpu.VMEM((4, 6, 8, Z), F32),
            pltpu.VMEM((n * rows, slots), F32),
            pltpu.VMEM((n * rows, slots), F32),
            pltpu.VMEM((n * back_rows, slots), F32),
            pltpu.VMEM((n * back_rows, slots), F32),
            pltpu.SemaphoreType.DMA((n,)),
            pltpu.SemaphoreType.DMA((n,)),
            pltpu.SemaphoreType.DMA((4,)),
            pltpu.SemaphoreType.DMA((4,)),
            pltpu.SemaphoreType.DMA((4,)),
            pltpu.SemaphoreType.DMA((4,)),
            pltpu.SemaphoreType.DMA((n,)),
            pltpu.SemaphoreType.DMA((n,)),
        ],
        compiler_params=pltpu.CompilerParams(collective_id=0, has_side_effects=True),
    )(
        flow_speed_field.reshape(3, X * Y, Z),
        thermal_field.reshape(X * Y, Z),
        walker_speed_vectors,
        walker_statistical_mass,
        gaussian_samples.reshape(6, blocks, slots),
        walker_strip_position,
        group_active_tally.reshape(1, blocks),
        group_resident_strip.reshape(1, blocks),
        migrating_group_table.reshape(1, moving),
        target_processor_slot.reshape(1, moving),
        entered_strip_slot.reshape(1, moving),
    )
    return fields.reshape(4, X, Y, Z), velocity


def solution(mesh):
    return jax.shard_map(
        shards,
        mesh=mesh,
        in_specs=(
            P(None, "gx", "yz", None),
            P("gx", "yz", None),
            P(None, ("gx", "yz"), None),
            P(("gx", "yz"), None),
            P(None, None, ("gx", "yz"), None),
            P(("gx", "yz"), None),
            P(("gx", "yz")),
            P(("gx", "yz")),
            P(("gx", "yz")),
            P(("gx", "yz"), None),
            P(("gx", "yz")),
        ),
        out_specs=(P(None, "gx", "yz", None), P(None, ("gx", "yz"), None)),
        check_vma=False,
    )
```

```python
import functools

import jax
import jax.numpy as jnp
from jax import lax
from jax.experimental import pallas as pl
from jax.experimental.pallas import tpu as pltpu
from jax.sharding import PartitionSpec as P

DECAY = 0.6
VISCOSITY = 0.05
COUPLING = 0.02
STRESS_GAIN = 0.005
RELAXATION = 0.5
PAIRS = ((0, 0), (0, 1), (0, 2), (1, 1), (1, 2), (2, 2))
PAIR_INDEX = ((0, 1, 2), (1, 3, 4), (2, 4, 5))
MOMENTS = 10
PITCH = 16
SENT = 9
LOAD_ORDER = (6, 7, 8, 9, 10, 0, 1, 5, 2, 3, 4)
MESH = pl.DeviceIdType.MESH
BF16 = jnp.bfloat16
F32 = jnp.float32


def split3(x):
    high = x.astype(BF16)
    rest = x - high.astype(F32)
    mid = rest.astype(BF16)
    low = (rest - mid.astype(F32)).astype(BF16)
    return high, mid, low


def dot(a, b):
    return jnp.dot(a, b, preferred_element_type=F32)


def dot_last(a, b):
    return lax.dot_general(a, b, (((1,), (1,)), ((), ())), preferred_element_type=F32)


def pick(onehot, x):
    high, mid, low = split3(x)
    return dot(onehot, high) + dot(onehot, mid) + dot(onehot, low)


def lanes(x, index):
    return jnp.take_along_axis(x, index, axis=1, mode="promise_in_bounds")


def onehot(condition):
    return jnp.where(condition, 1.0, 0.0)


def drift(start, u, spread, noise):
    return u + DECAY * (start - u) + spread * noise


def deposit(count, unroll, v_ref, cells_ref, pb_ref):
    width = v_ref.shape[1]
    slots = cells_ref.shape[1]
    where = lax.broadcasted_iota(jnp.int32, (width, slots), 0)

    def some(step, carry):
        for t in range(unroll):
            n = step * unroll + t
            row = pl.ds(pl.multiple_of(n * PITCH, PITCH), PITCH)
            lhs = jnp.concatenate(split3(v_ref[row, :]), axis=0)
            hot = onehot(cells_ref[pl.ds(n, 1), :] == where).astype(BF16)
            out = dot_last(lhs, hot)
            pb_ref[row, :] = out[:PITCH] + out[PITCH : 2 * PITCH] + out[2 * PITCH :]
        return carry

    lax.fori_loop(0, count // unroll, some, 0)


def put_terms(v_ref, count, weight, second):
    terms = (
        [weight]
        + [weight * second[row] for row in range(3)]
        + [weight * second[one] * second[two] for one, two in PAIRS]
    )
    for k, term in enumerate(terms):
        v_ref[pl.ds(k, count, stride=PITCH), :] = term


def kernel(
    n,
    n_gx,
    spans,
    *refs,
):
    sources, (fields_out, speed_out), held, load_s = refs[:11], refs[11:13], refs[13:24], refs[24]
    flow, heat, speed, mass, noise, cells, tally, home, table, target, entered = held
    (
    v_ref,
    pb_ref,
    second_ref,
    cells_a,
    moments,
    wide,
    face_send,
    face_recv,
    stress_send,
    stress_recv,
    out_ref,
    in_ref,
    back_send,
    back_recv,
    out_s,
    out_r,
    face_s,
    face_r,
    stress_s,
    stress_r,
    back_s,
    back_r,
    ) = refs[25:]
    loads = [
        pltpu.make_async_copy(source, kept, load_s.at[i])
        for i, (source, kept) in enumerate(zip(sources, held))
    ]
    X, Y, Z = spans
    pencils = X * Y
    blocks, slots = mass.shape
    moving = table.shape[1]
    cap = 2 * moving // n
    received = n * cap
    rows = out_ref.shape[0] // n
    back_rows = back_send.shape[0] // n
    gx = lax.axis_index("gx")
    me = lax.axis_index("yz")
    order = sorted(range(1, n), key=lambda i: abs(2 * i - n))
    peers = [(i, lax.rem(me + i, n), lax.rem(me + n - i, n)) for i in order]
    for i in LOAD_ORDER:
        loads[i].start()

    barrier = pltpu.get_barrier_semaphore()
    for _, peer, _ in peers:
        pl.semaphore_signal(barrier, inc=1, device_id={"yz": peer}, device_id_type=MESH)

    @pl.when(gx > 0)
    def _():
        pl.semaphore_signal(barrier, inc=1, device_id={"gx": gx - 1}, device_id_type=MESH)

    @pl.when(gx < n_gx - 1)
    def _():
        pl.semaphore_signal(barrier, inc=1, device_id={"gx": gx + 1}, device_id_type=MESH)

    sides = (
        (0, 1, gx > 0, gx == 0, {"gx": gx - 1}),
        (1, 0, gx < n_gx - 1, gx == n_gx - 1, {"gx": gx + 1}),
        (2, 3, me > 0, me == 0, {"yz": me - 1}),
        (3, 2, me < n - 1, me == n - 1, {"yz": me + 1}),
    )
    for side, _, _, edge, _ in sides:

        @pl.when(edge)
        def _(side=side):
            face_recv[side] = jnp.zeros(face_recv.shape[1:], F32)
            stress_recv[side] = jnp.zeros(stress_recv.shape[1:], F32)

    def face_copy(side, other, where, send, recv, send_sem, recv_sem):
        return pltpu.make_async_remote_copy(
            src_ref=send.at[side],
            dst_ref=recv.at[other],
            send_sem=send_sem.at[side],
            recv_sem=recv_sem.at[other],
            device_id=where,
            device_id_type=MESH,
        )

    def faces_start(send, recv, send_sem, recv_sem):
        for side, other, there, _, where in sides:

            @pl.when(there)
            def _(side=side, other=other, where=where):
                face_copy(side, other, where, send, recv, send_sem, recv_sem).start()

    def faces_wait(send, recv, send_sem, recv_sem):
        for side, _, there, _, where in sides:

            @pl.when(there)
            def _(side=side, where=where):
                face_copy(side, side, where, send, recv, send_sem, recv_sem).wait_recv()

    def faces_sent(send, recv, send_sem, recv_sem):
        for side, other, there, _, where in sides:

            @pl.when(there)
            def _(side=side, other=other, where=where):
                face_copy(side, other, where, send, recv, send_sem, recv_sem).wait_send()

    face_args = (face_send, face_recv, face_s, face_r)
    stress_args = (stress_send, stress_recv, stress_s, stress_r)

    def all_copy(i, peer, send, recv, height, send_sem, recv_sem):
        return pltpu.make_async_remote_copy(
            src_ref=send.at[pl.ds(pl.multiple_of(peer * height, 8), height), :],
            dst_ref=recv.at[pl.ds(pl.multiple_of(me * height, 8), height), :],
            send_sem=send_sem.at[i],
            recv_sem=recv_sem.at[i],
            device_id={"yz": peer},
            device_id_type=MESH,
        )

    def all_start(send, recv, height, send_sem, recv_sem):
        for i, peer, _ in peers:
            all_copy(i, peer, send, recv, height, send_sem, recv_sem).start()

    def all_wait(send, recv, height, send_sem, recv_sem):
        for i, _, source in peers:
            pltpu.make_async_remote_copy(
                src_ref=send.at[pl.ds(pl.multiple_of(source * height, 8), height), :],
                dst_ref=recv.at[pl.ds(pl.multiple_of(source * height, 8), height), :],
                send_sem=send_sem.at[i],
                recv_sem=recv_sem.at[i],
                device_id={"yz": source},
                device_id_type=MESH,
            ).wait_recv()

    def all_sent(send, recv, height, send_sem, recv_sem):
        for i, peer, _ in peers:
            all_copy(i, peer, send, recv, height, send_sem, recv_sem).wait_send()

    pay_args = (out_ref, in_ref, rows, out_s, out_r)
    back_args = (back_send, back_recv, back_rows, back_s, back_r)

    for load in loads:
        load.wait()

    for c in range(4):
        grid = flow.at[c] if c < 3 else heat
        face_send[0, c] = grid[pl.ds(0, Y), :]
        face_send[1, c] = grid[pl.ds((X - 1) * Y, Y), :]
        face_send[2, c] = grid[pl.ds(0, X, stride=Y), :]
        face_send[3, c] = grid[pl.ds(Y - 1, X, stride=Y), :]

    iota = functools.partial(lax.broadcasted_iota, jnp.int32)
    eye = iota((moving, moving), 0) == iota((moving, moving), 1)
    target_row = target[...]
    target_col = jnp.sum(jnp.where(eye, target_row, 0), axis=1, keepdims=True)
    earlier = (target_col == target_row) & (iota((moving, moving), 0) < iota((moving, moving), 1))
    rank = jnp.sum(jnp.where(earlier, 1, 0), axis=0, keepdims=True)
    slot_row = rank * n + target_row
    slot_hot = onehot(iota((received, moving), 0) == slot_row)
    block_hot = onehot(iota((blocks, moving), 0) == table[...])
    from_block = dot_last(slot_hot.astype(BF16), block_hot.astype(BF16)).astype(BF16)
    to_block = dot_last(block_hot.astype(BF16), slot_hot.astype(BF16))
    moved = jnp.sum(to_block, axis=1, keepdims=True) > 0.5
    to_block = to_block.astype(BF16)
    pencil_out = jnp.sum(slot_hot * entered[...].astype(F32), axis=1, keepdims=True)

    home_t = onehot(iota((pencils, blocks), 0) == home[...])
    home_hot = home_t.T.astype(BF16)
    home_t = home_t.astype(BF16)
    live = onehot(iota((slots, blocks), 0) < tally[...]).T

    where = cells[...]
    u = [lanes(pick(home_hot, flow[c]), where) for c in range(3)]
    temp = lanes(pick(home_hot, heat[...]), where)
    spread = jnp.sqrt((1.0 - DECAY * DECAY) * temp)
    weight = mass[...] * live
    first = [drift(speed[c], u[c], spread, noise[c]) for c in range(3)]
    sent = [pick(from_block, first[c]) for c in range(3)]
    sent.append(pick(from_block, weight))
    sent += [pick(from_block, noise[3 + c]) for c in range(3)]
    sent.append(dot(from_block, where.astype(F32).astype(BF16)))
    sent.append(jnp.broadcast_to(pencil_out, (received, slots)))
    for c in range(SENT):
        for j in range(cap):
            out_ref[pl.ds(c * cap + j, n, stride=rows), :] = sent[c][j * n : (j + 1) * n]

    expected = n - 1 + jnp.where(gx > 0, 1, 0) + jnp.where(gx < n_gx - 1, 1, 0)
    pl.semaphore_wait(barrier, expected)
    all_start(*pay_args)
    faces_start(*face_args)
    own = pl.ds(pl.multiple_of(me * rows, 8), rows)
    in_ref[own, :] = out_ref[own, :]

    second = [drift(first[c], u[c], spread, noise[3 + c]) for c in range(3)]
    for c in range(3):
        second_ref[c] = second[c]
    put_terms(v_ref, blocks, jnp.where(moved, 0.0, weight), second)
    deposit(blocks, 8, v_ref, cells, pb_ref)
    for k in range(MOMENTS):
        moments[k] = pick(home_t, pb_ref[pl.ds(k, blocks, stride=PITCH), :])

    all_wait(*pay_args)
    got = [
        jnp.concatenate(
            [in_ref[pl.ds(c * cap + j, n, stride=rows), :] for j in range(cap)], axis=0
        )
        for c in range(SENT)
    ]
    where_a = got[7].astype(jnp.int32)
    cells_a[...] = where_a
    pencil_hot = onehot(got[8][:, :pencils].astype(jnp.int32) == iota((received, pencils), 1))
    pencil_t = pencil_hot.T.astype(BF16)
    pencil_hot = pencil_hot.astype(BF16)
    u_a = [lanes(pick(pencil_hot, flow[c]), where_a) for c in range(3)]
    temp_a = lanes(pick(pencil_hot, heat[...]), where_a)
    spread_a = jnp.sqrt((1.0 - DECAY * DECAY) * temp_a)
    second_a = [drift(got[c], u_a[c], spread_a, got[4 + c]) for c in range(3)]
    put_terms(v_ref, received, got[3], second_a)
    deposit(received, 8, v_ref, cells_a, pb_ref)
    for k in range(MOMENTS - 1, -1, -1):
        total = moments[k] + pick(pencil_t, pb_ref[pl.ds(k, received, stride=PITCH), :])
        moments[k] = total
        if k >= 4:
            s = k - 4
            stress_send[0, s] = total[:Y]
            stress_send[1, s] = total[pencils - Y :]
            stress_send[2, s] = moments[k, pl.ds(0, X, stride=Y), :]
            stress_send[3, s] = moments[k, pl.ds(Y - 1, X, stride=Y), :]
    faces_start(*stress_args)

    lane = iota((pencils, Z), 1)

    def along_z(x, step):
        if step > 0:
            return jnp.where(lane == Z - 1, 0.0, pltpu.roll(x, Z - 1, 1))
        return jnp.where(lane == 0, 0.0, pltpu.roll(x, 1, 1))

    def fill(slot, value, halo, c):
        wide[slot, 1 : X + 1, 8 : 8 + Y, :] = value.reshape(X, Y, Z)
        wide[slot, 0, 8 : 8 + Y, :] = halo[0, c]
        wide[slot, X + 1, 8 : 8 + Y, :] = halo[1, c]
        for x in range(X):
            wide[slot, x + 1, 7:8, :] = halo[2, c, x : x + 1]
            wide[slot, x + 1, 8 + Y : 9 + Y, :] = halo[3, c, x : x + 1]

    def along_x(slot, step):
        return wide[slot, 1 + step : 1 + step + X, 8 : 8 + Y, :].reshape(pencils, Z)

    def along_y(slot, step):
        return wide[slot, 1 : X + 1, 8 + step : 8 + step + Y, :].reshape(pencils, Z)

    faces_wait(*face_args)
    f = [flow[0], flow[1], flow[2], heat[...]]
    base = []
    for c in range(4):
        fill(c, f[c], face_recv, c)
        smooth = along_x(c, 1) + along_x(c, -1) + along_y(c, 1) + along_y(c, -1)
        smooth = smooth + along_z(f[c], 1) + along_z(f[c], -1) - 6.0 * f[c]
        base.append(f[c] + VISCOSITY * smooth)
    density = moments[0]
    momentum = [moments[1 + c] for c in range(3)]
    for c in range(3):
        base[c] = base[c] + COUPLING * (momentum[c] - density * f[c])
    dots = momentum[0] * f[0] + momentum[1] * f[1] + momentum[2] * f[2]
    squares = f[0] * f[0] + f[1] * f[1] + f[2] * f[2]
    energy = (moments[4] + moments[7] + moments[9] - 2.0 * dots + density * squares) / 3.0
    fields_out[3] = base[3] + COUPLING * (energy - density * f[3])
    stress = [moments[4 + s] for s in range(6)]
    slope_z = [along_z(stress[s], 1) - along_z(stress[s], -1) for s in (2, 4, 5)]

    faces_wait(*stress_args)
    for s in range(6):
        if s < 5:
            fill(4 + s, stress[s], stress_recv, s)
    fresh = []
    for row in range(3):
        sx, sy, _ = PAIR_INDEX[row]
        slope = along_x(4 + sx, 1) - along_x(4 + sx, -1) + slope_z[row]
        slope = slope + along_y(4 + sy, 1) - along_y(4 + sy, -1)
        value = base[row] - (0.5 * STRESS_GAIN) * slope
        fields_out[row] = value
        fresh.append(split3(value))

    def sampled(hot, c):
        return dot(hot, fresh[c][0]) + dot(hot, fresh[c][1]) + dot(hot, fresh[c][2])

    for c in range(3):
        w = lanes(sampled(pencil_hot, c), where_a)
        third = second_a[c] + RELAXATION * (w - second_a[c])
        for j in range(cap):
            back_send[pl.ds(c * cap + j, n, stride=back_rows), :] = third[j * n : (j + 1) * n]
    all_start(*back_args)
    own = pl.ds(pl.multiple_of(me * back_rows, 8), back_rows)
    back_recv[own, :] = back_send[own, :]
    for c in range(3):
        w = lanes(sampled(home_hot, c), where)
        now = second_ref[c]
        second_ref[c] = live * (now + RELAXATION * (w - now))
    all_wait(*back_args)
    for c in range(3):
        returned = jnp.concatenate(
            [back_recv[pl.ds(c * cap + j, n, stride=back_rows), :] for j in range(cap)], axis=0
        )
        speed_out[c] = jnp.where(moved, live * pick(to_block, returned), second_ref[c])

    all_sent(*pay_args)
    faces_sent(*face_args)
    faces_sent(*stress_args)
    all_sent(*back_args)


def shards(
    flow_speed_field,
    thermal_field,
    walker_speed_vectors,
    walker_statistical_mass,
    gaussian_samples,
    walker_strip_position,
    group_active_tally,
    group_resident_strip,
    migrating_group_table,
    target_processor_slot,
    entered_strip_slot,
):
    n = lax.axis_size("yz")
    n_gx = lax.axis_size("gx")
    X, Y, Z = thermal_field.shape
    blocks, slots = walker_statistical_mass.shape
    moving = migrating_group_table.shape[0]
    cap = 2 * moving // n
    received = n * cap
    rows = -(-SENT * cap // 8) * 8
    back_rows = -(-3 * cap // 8) * 8
    operands = (
        flow_speed_field.reshape(3, X * Y, Z),
        thermal_field.reshape(X * Y, Z),
        walker_speed_vectors,
        walker_statistical_mass,
        gaussian_samples.reshape(6, blocks, slots),
        walker_strip_position,
        group_active_tally.reshape(1, blocks),
        group_resident_strip.reshape(1, blocks),
        migrating_group_table.reshape(1, moving),
        target_processor_slot.reshape(1, moving),
        entered_strip_slot.reshape(1, moving),
    )
    vmem = pl.BlockSpec(memory_space=pltpu.VMEM)
    fields, velocity = pl.pallas_call(
        functools.partial(kernel, n, n_gx, (X, Y, Z)),
        out_shape=(
            pltpu.VMEM((4, X * Y, Z), F32),
            pltpu.VMEM((3, blocks, slots), F32),
        ),
        in_specs=[pl.BlockSpec(memory_space=pltpu.HBM)] * 11,
        out_specs=(vmem, vmem),
        scratch_shapes=[pltpu.VMEM(x.shape, x.dtype) for x in operands]
        + [pltpu.SemaphoreType.DMA((11,))]
        + [
            pltpu.VMEM((max(blocks, received) * PITCH, slots), F32),
            pltpu.VMEM((max(blocks, received) * PITCH, Z), F32),
            pltpu.VMEM((3, blocks, slots), F32),
            pltpu.VMEM((received, slots), jnp.int32),
            pltpu.VMEM((MOMENTS, X * Y, Z), F32),
            pltpu.VMEM((9, X + 2, 24, Z), F32),
            pltpu.VMEM((4, 4, 8, Z), F32),
            pltpu.VMEM((4, 4, 8, Z), F32),
            pltpu.VMEM((4, 6, 8, Z), F32),
            pltpu.VMEM((4, 6, 8, Z), F32),
            pltpu.VMEM((n * rows, slots), F32),
            pltpu.VMEM((n * rows, slots), F32),
            pltpu.VMEM((n * back_rows, slots), F32),
            pltpu.VMEM((n * back_rows, slots), F32),
            pltpu.SemaphoreType.DMA((n,)),
            pltpu.SemaphoreType.DMA((n,)),
            pltpu.SemaphoreType.DMA((4,)),
            pltpu.SemaphoreType.DMA((4,)),
            pltpu.SemaphoreType.DMA((4,)),
            pltpu.SemaphoreType.DMA((4,)),
            pltpu.SemaphoreType.DMA((n,)),
            pltpu.SemaphoreType.DMA((n,)),
        ],
        compiler_params=pltpu.CompilerParams(
            collective_id=0, has_side_effects=True, vmem_limit_bytes=32 * 1024 * 1024
        ),
    )(*(pltpu.with_memory_space_constraint(x, pltpu.HBM) for x in operands))
    return fields.reshape(4, X, Y, Z), velocity


def solution(mesh):
    return jax.shard_map(
        shards,
        mesh=mesh,
        in_specs=(
            P(None, "gx", "yz", None),
            P("gx", "yz", None),
            P(None, ("gx", "yz"), None),
            P(("gx", "yz"), None),
            P(None, None, ("gx", "yz"), None),
            P(("gx", "yz"), None),
            P(("gx", "yz")),
            P(("gx", "yz")),
            P(("gx", "yz")),
            P(("gx", "yz"), None),
            P(("gx", "yz")),
        ),
        out_specs=(P(None, "gx", "yz", None), P(None, ("gx", "yz"), None)),
        check_vma=False,
    )
```

```python
import functools
import math

import jax
import jax.numpy as jnp
from jax import lax
from jax.experimental import pallas as pl
from jax.experimental.pallas import tpu as pltpu
from jax.sharding import PartitionSpec as P

DECAY = 0.6
VISCOSITY = 0.05
COUPLING = 0.02
STRESS_GAIN = 0.005
RELAXATION = 0.5
PAIRS = ((0, 0), (0, 1), (0, 2), (1, 1), (1, 2), (2, 2))
PAIR_INDEX = ((0, 1, 2), (1, 3, 4), (2, 4, 5))
MOMENTS = 10
PITCH = 16
SENT = 9
UNROLL = 32
LOAD_ORDER = (6, 7, 8, 9, 10, 0, 1, 5, 2, 3, 4)
MESH = pl.DeviceIdType.MESH
BF16 = jnp.bfloat16
F32 = jnp.float32


def split3(x):
    high = x.astype(BF16)
    rest = x - high.astype(F32)
    mid = rest.astype(BF16)
    low = (rest - mid.astype(F32)).astype(BF16)
    return high, mid, low


def dot(a, b):
    return jnp.dot(a, b, preferred_element_type=F32)


def dot_last(a, b):
    return lax.dot_general(a, b, (((1,), (1,)), ((), ())), preferred_element_type=F32)


def pick(onehot, x):
    high, mid, low = split3(x)
    return dot(onehot, high) + dot(onehot, mid) + dot(onehot, low)


def lanes(x, index):
    return jnp.take_along_axis(x, index, axis=1, mode="promise_in_bounds")


def onehot(condition):
    return jnp.where(condition, 1.0, 0.0)


def drift(start, u, spread, noise):
    return u + DECAY * (start - u) + spread * noise


def deposit(count, unroll, v_ref, cells_ref, pb_ref):
    width = v_ref.shape[1]
    slots = cells_ref.shape[1]
    where = lax.broadcasted_iota(jnp.int32, (width, slots), 0)

    def some(step, carry):
        for t in range(unroll):
            n = step * unroll + t
            row = pl.ds(pl.multiple_of(n * PITCH, PITCH), PITCH)
            lhs = jnp.concatenate(split3(v_ref[row, :]), axis=0)
            hot = onehot(cells_ref[pl.ds(n, 1), :] == where).astype(BF16)
            out = dot_last(lhs, hot)
            pb_ref[row, :] = out[:PITCH] + out[PITCH : 2 * PITCH] + out[2 * PITCH :]
        return carry

    lax.fori_loop(0, count // unroll, some, 0)


def put_terms(v_ref, count, weight, second):
    terms = (
        [weight]
        + [weight * second[row] for row in range(3)]
        + [weight * second[one] * second[two] for one, two in PAIRS]
    )
    for k, term in enumerate(terms):
        v_ref[pl.ds(k, count, stride=PITCH), :] = term


def kernel(
    n,
    n_gx,
    spans,
    *refs,
):
    sources, (fields_out, speed_out), held, load_s = refs[:11], refs[11:13], refs[13:24], refs[24]
    flow, heat, speed, mass, noise, cells, tally, home, table, target, entered = held
    (
    v_ref,
    pb_ref,
    second_ref,
    cells_a,
    moments,
    wide,
    face_send,
    face_recv,
    stress_send,
    stress_recv,
    out_ref,
    in_ref,
    back_send,
    back_recv,
    out_s,
    out_r,
    face_s,
    face_r,
    stress_s,
    stress_r,
    back_s,
    back_r,
    ) = refs[25:]
    loads = [
        pltpu.make_async_copy(source, kept, load_s.at[i])
        for i, (source, kept) in enumerate(zip(sources, held))
    ]
    X, Y, Z = spans
    pencils = X * Y
    blocks, slots = mass.shape
    moving = table.shape[1]
    cap = 2 * moving // n
    received = n * cap
    rows = out_ref.shape[0] // n
    back_rows = back_send.shape[0] // n
    gx = lax.axis_index("gx")
    me = lax.axis_index("yz")
    order = sorted(range(1, n), key=lambda i: abs(2 * i - n))
    peers = [(i, lax.rem(me + i, n), lax.rem(me + n - i, n)) for i in order]
    for i in LOAD_ORDER:
        loads[i].start()

    barrier = pltpu.get_barrier_semaphore()
    for _, peer, _ in peers:
        pl.semaphore_signal(barrier, inc=1, device_id={"yz": peer}, device_id_type=MESH)

    @pl.when(gx > 0)
    def _():
        pl.semaphore_signal(barrier, inc=1, device_id={"gx": gx - 1}, device_id_type=MESH)

    @pl.when(gx < n_gx - 1)
    def _():
        pl.semaphore_signal(barrier, inc=1, device_id={"gx": gx + 1}, device_id_type=MESH)

    sides = (
        (0, 1, gx > 0, gx == 0, {"gx": gx - 1}),
        (1, 0, gx < n_gx - 1, gx == n_gx - 1, {"gx": gx + 1}),
        (2, 3, me > 0, me == 0, {"yz": me - 1}),
        (3, 2, me < n - 1, me == n - 1, {"yz": me + 1}),
    )
    for side, _, _, edge, _ in sides:

        @pl.when(edge)
        def _(side=side):
            face_recv[side] = jnp.zeros(face_recv.shape[1:], F32)
            stress_recv[side] = jnp.zeros(stress_recv.shape[1:], F32)

    def face_copy(side, other, where, send, recv, send_sem, recv_sem):
        return pltpu.make_async_remote_copy(
            src_ref=send.at[side],
            dst_ref=recv.at[other],
            send_sem=send_sem.at[side],
            recv_sem=recv_sem.at[other],
            device_id=where,
            device_id_type=MESH,
        )

    def faces_start(send, recv, send_sem, recv_sem):
        for side, other, there, _, where in sides:

            @pl.when(there)
            def _(side=side, other=other, where=where):
                face_copy(side, other, where, send, recv, send_sem, recv_sem).start()

    def faces_wait(send, recv, send_sem, recv_sem):
        for side, _, there, _, where in sides:

            @pl.when(there)
            def _(side=side, where=where):
                face_copy(side, side, where, send, recv, send_sem, recv_sem).wait_recv()

    def faces_sent(send, recv, send_sem, recv_sem):
        for side, other, there, _, where in sides:

            @pl.when(there)
            def _(side=side, other=other, where=where):
                face_copy(side, other, where, send, recv, send_sem, recv_sem).wait_send()

    face_args = (face_send, face_recv, face_s, face_r)
    stress_args = (stress_send, stress_recv, stress_s, stress_r)

    def all_copy(i, peer, send, recv, height, pitch, send_sem, recv_sem):
        return pltpu.make_async_remote_copy(
            src_ref=send.at[pl.ds(pl.multiple_of(peer * pitch, 8), height), :],
            dst_ref=recv.at[pl.ds(pl.multiple_of(me * pitch, 8), height), :],
            send_sem=send_sem.at[i],
            recv_sem=recv_sem.at[i],
            device_id={"yz": peer},
            device_id_type=MESH,
        )

    def all_start(send, recv, height, pitch, send_sem, recv_sem):
        for i, peer, _ in peers:
            all_copy(i, peer, send, recv, height, pitch, send_sem, recv_sem).start()

    def all_wait(send, recv, height, pitch, send_sem, recv_sem):
        for i, _, source in peers:
            pltpu.make_async_remote_copy(
                src_ref=send.at[pl.ds(pl.multiple_of(source * pitch, 8), height), :],
                dst_ref=recv.at[pl.ds(pl.multiple_of(source * pitch, 8), height), :],
                send_sem=send_sem.at[i],
                recv_sem=recv_sem.at[i],
                device_id={"yz": source},
                device_id_type=MESH,
            ).wait_recv()

    def all_sent(send, recv, height, pitch, send_sem, recv_sem):
        for i, peer, _ in peers:
            all_copy(i, peer, send, recv, height, pitch, send_sem, recv_sem).wait_send()

    pay_args = (out_ref, in_ref, SENT * cap, rows, out_s, out_r)
    back_args = (back_send, back_recv, 3 * cap, back_rows, back_s, back_r)

    for load in loads:
        load.wait()

    for c in range(4):
        grid = flow.at[c] if c < 3 else heat
        face_send[0, c] = grid[pl.ds(0, Y), :]
        face_send[1, c] = grid[pl.ds((X - 1) * Y, Y), :]
        face_send[2, c] = grid[pl.ds(0, X, stride=Y), :]
        face_send[3, c] = grid[pl.ds(Y - 1, X, stride=Y), :]

    iota = functools.partial(lax.broadcasted_iota, jnp.int32)
    eye = iota((moving, moving), 0) == iota((moving, moving), 1)
    target_row = target[...]
    target_col = jnp.sum(jnp.where(eye, target_row, 0), axis=1, keepdims=True)
    earlier = (target_col == target_row) & (iota((moving, moving), 0) < iota((moving, moving), 1))
    rank = jnp.sum(jnp.where(earlier, 1, 0), axis=0, keepdims=True)
    slot_row = rank * n + target_row
    slot_hot = onehot(iota((received, moving), 0) == slot_row)
    block_hot = onehot(iota((blocks, moving), 0) == table[...])
    from_block = dot_last(slot_hot.astype(BF16), block_hot.astype(BF16)).astype(BF16)
    to_block = dot_last(block_hot.astype(BF16), slot_hot.astype(BF16))
    moved = jnp.sum(to_block, axis=1, keepdims=True) > 0.5
    to_block = to_block.astype(BF16)
    pencil_out = jnp.sum(slot_hot * entered[...].astype(F32), axis=1, keepdims=True)

    home_t = onehot(iota((pencils, blocks), 0) == home[...])
    home_hot = home_t.T.astype(BF16)
    home_t = home_t.astype(BF16)
    live = onehot(iota((slots, blocks), 0) < tally[...]).T

    where = cells[...]
    u = [lanes(pick(home_hot, flow[c]), where) for c in range(3)]
    temp = lanes(pick(home_hot, heat[...]), where)
    spread = jnp.sqrt((1.0 - DECAY * DECAY) * temp)
    weight = mass[...] * live
    first = [drift(speed[c], u[c], spread, noise[c]) for c in range(3)]
    sent = [pick(from_block, first[c]) for c in range(3)]
    sent.append(pick(from_block, weight))
    sent += [pick(from_block, noise[3 + c]) for c in range(3)]
    sent.append(dot(from_block, where.astype(F32).astype(BF16)))
    sent.append(jnp.broadcast_to(pencil_out, (received, slots)))
    for c in range(SENT):
        for j in range(cap):
            out_ref[pl.ds(c * cap + j, n, stride=rows), :] = sent[c][j * n : (j + 1) * n]

    expected = n - 1 + jnp.where(gx > 0, 1, 0) + jnp.where(gx < n_gx - 1, 1, 0)
    pl.semaphore_wait(barrier, expected)
    all_start(*pay_args)
    faces_start(*face_args)
    own = pl.ds(pl.multiple_of(me * rows, 8), rows)
    in_ref[own, :] = out_ref[own, :]

    second = [drift(first[c], u[c], spread, noise[3 + c]) for c in range(3)]
    for c in range(3):
        second_ref[c] = second[c]
    put_terms(v_ref, blocks, jnp.where(moved, 0.0, weight), second)
    deposit(blocks, math.gcd(blocks, UNROLL), v_ref, cells, pb_ref)
    for k in range(MOMENTS):
        moments[k] = pick(home_t, pb_ref[pl.ds(k, blocks, stride=PITCH), :])

    all_wait(*pay_args)
    got = [
        jnp.concatenate(
            [in_ref[pl.ds(c * cap + j, n, stride=rows), :] for j in range(cap)], axis=0
        )
        for c in range(SENT)
    ]
    where_a = got[7].astype(jnp.int32)
    cells_a[...] = where_a
    pencil_hot = onehot(got[8][:, :pencils].astype(jnp.int32) == iota((received, pencils), 1))
    pencil_t = pencil_hot.T.astype(BF16)
    pencil_hot = pencil_hot.astype(BF16)
    u_a = [lanes(pick(pencil_hot, flow[c]), where_a) for c in range(3)]
    temp_a = lanes(pick(pencil_hot, heat[...]), where_a)
    spread_a = jnp.sqrt((1.0 - DECAY * DECAY) * temp_a)
    second_a = [drift(got[c], u_a[c], spread_a, got[4 + c]) for c in range(3)]
    put_terms(v_ref, received, got[3], second_a)
    deposit(received, math.gcd(received, UNROLL), v_ref, cells_a, pb_ref)
    for k in range(MOMENTS - 1, -1, -1):
        total = moments[k] + pick(pencil_t, pb_ref[pl.ds(k, received, stride=PITCH), :])
        moments[k] = total
        if k >= 4:
            s = k - 4
            stress_send[0, s] = total[:Y]
            stress_send[1, s] = total[pencils - Y :]
            stress_send[2, s] = moments[k, pl.ds(0, X, stride=Y), :]
            stress_send[3, s] = moments[k, pl.ds(Y - 1, X, stride=Y), :]
    faces_start(*stress_args)

    lane = iota((pencils, Z), 1)

    def along_z(x, step):
        if step > 0:
            return jnp.where(lane == Z - 1, 0.0, pltpu.roll(x, Z - 1, 1))
        return jnp.where(lane == 0, 0.0, pltpu.roll(x, 1, 1))

    def fill(slot, value, halo, c):
        wide[slot, 1 : X + 1, 8 : 8 + Y, :] = value.reshape(X, Y, Z)
        wide[slot, 0, 8 : 8 + Y, :] = halo[0, c]
        wide[slot, X + 1, 8 : 8 + Y, :] = halo[1, c]
        for x in range(X):
            wide[slot, x + 1, 7:8, :] = halo[2, c, x : x + 1]
            wide[slot, x + 1, 8 + Y : 9 + Y, :] = halo[3, c, x : x + 1]

    def along_x(slot, step):
        return wide[slot, 1 + step : 1 + step + X, 8 : 8 + Y, :].reshape(pencils, Z)

    def along_y(slot, step):
        return wide[slot, 1 : X + 1, 8 + step : 8 + step + Y, :].reshape(pencils, Z)

    faces_wait(*face_args)
    f = [flow[0], flow[1], flow[2], heat[...]]
    base = []
    for c in range(4):
        fill(c, f[c], face_recv, c)
        smooth = along_x(c, 1) + along_x(c, -1) + along_y(c, 1) + along_y(c, -1)
        smooth = smooth + along_z(f[c], 1) + along_z(f[c], -1) - 6.0 * f[c]
        base.append(f[c] + VISCOSITY * smooth)
    density = moments[0]
    momentum = [moments[1 + c] for c in range(3)]
    for c in range(3):
        base[c] = base[c] + COUPLING * (momentum[c] - density * f[c])
    dots = momentum[0] * f[0] + momentum[1] * f[1] + momentum[2] * f[2]
    squares = f[0] * f[0] + f[1] * f[1] + f[2] * f[2]
    energy = (moments[4] + moments[7] + moments[9] - 2.0 * dots + density * squares) / 3.0
    fields_out[3] = base[3] + COUPLING * (energy - density * f[3])
    stress = [moments[4 + s] for s in range(6)]
    slope_z = [along_z(stress[s], 1) - along_z(stress[s], -1) for s in (2, 4, 5)]

    faces_wait(*stress_args)
    for s in range(6):
        if s < 5:
            fill(4 + s, stress[s], stress_recv, s)
    fresh = []
    for row in range(3):
        sx, sy, _ = PAIR_INDEX[row]
        slope = along_x(4 + sx, 1) - along_x(4 + sx, -1) + slope_z[row]
        slope = slope + along_y(4 + sy, 1) - along_y(4 + sy, -1)
        value = base[row] - (0.5 * STRESS_GAIN) * slope
        fields_out[row] = value
        fresh.append(split3(value))

    def sampled(hot, c):
        return dot(hot, fresh[c][0]) + dot(hot, fresh[c][1]) + dot(hot, fresh[c][2])

    for c in range(3):
        w = lanes(sampled(pencil_hot, c), where_a)
        third = second_a[c] + RELAXATION * (w - second_a[c])
        for j in range(cap):
            back_send[pl.ds(c * cap + j, n, stride=back_rows), :] = third[j * n : (j + 1) * n]
    all_start(*back_args)
    own = pl.ds(pl.multiple_of(me * back_rows, 8), back_rows)
    back_recv[own, :] = back_send[own, :]
    for c in range(3):
        w = lanes(sampled(home_hot, c), where)
        now = second_ref[c]
        second_ref[c] = live * (now + RELAXATION * (w - now))
    all_wait(*back_args)
    for c in range(3):
        returned = jnp.concatenate(
            [back_recv[pl.ds(c * cap + j, n, stride=back_rows), :] for j in range(cap)], axis=0
        )
        speed_out[c] = jnp.where(moved, live * pick(to_block, returned), second_ref[c])

    all_sent(*pay_args)
    faces_sent(*face_args)
    faces_sent(*stress_args)
    all_sent(*back_args)


def put_out(fields, velocity, fields_out, velocity_out, sems):
    copies = (
        pltpu.make_async_copy(fields, fields_out, sems.at[0]),
        pltpu.make_async_copy(velocity, velocity_out, sems.at[1]),
    )
    for copy in copies:
        copy.start()
    for copy in copies:
        copy.wait()


def shards(
    flow_speed_field,
    thermal_field,
    walker_speed_vectors,
    walker_statistical_mass,
    gaussian_samples,
    walker_strip_position,
    group_active_tally,
    group_resident_strip,
    migrating_group_table,
    target_processor_slot,
    entered_strip_slot,
):
    n = lax.axis_size("yz")
    n_gx = lax.axis_size("gx")
    X, Y, Z = thermal_field.shape
    blocks, slots = walker_statistical_mass.shape
    moving = migrating_group_table.shape[0]
    cap = 2 * moving // n
    received = n * cap
    rows = -(-SENT * cap // 8) * 8
    back_rows = -(-3 * cap // 8) * 8
    operands = (
        flow_speed_field.reshape(3, X * Y, Z),
        thermal_field.reshape(X * Y, Z),
        walker_speed_vectors,
        walker_statistical_mass,
        gaussian_samples.reshape(6, blocks, slots),
        walker_strip_position,
        group_active_tally.reshape(1, blocks),
        group_resident_strip.reshape(1, blocks),
        migrating_group_table.reshape(1, moving),
        target_processor_slot.reshape(1, moving),
        entered_strip_slot.reshape(1, moving),
    )
    vmem = pl.BlockSpec(memory_space=pltpu.VMEM)
    fields, velocity = pl.pallas_call(
        functools.partial(kernel, n, n_gx, (X, Y, Z)),
        out_shape=(
            pltpu.VMEM((4, X * Y, Z), F32),
            pltpu.VMEM((3, blocks, slots), F32),
        ),
        in_specs=[pl.BlockSpec(memory_space=pltpu.HBM)] * 11,
        out_specs=(vmem, vmem),
        scratch_shapes=[pltpu.VMEM(x.shape, x.dtype) for x in operands]
        + [pltpu.SemaphoreType.DMA((11,))]
        + [
            pltpu.VMEM((max(blocks, received) * PITCH, slots), F32),
            pltpu.VMEM((max(blocks, received) * PITCH, Z), F32),
            pltpu.VMEM((3, blocks, slots), F32),
            pltpu.VMEM((received, slots), jnp.int32),
            pltpu.VMEM((MOMENTS, X * Y, Z), F32),
            pltpu.VMEM((9, X + 2, 24, Z), F32),
            pltpu.VMEM((4, 4, 8, Z), F32),
            pltpu.VMEM((4, 4, 8, Z), F32),
            pltpu.VMEM((4, 6, 8, Z), F32),
            pltpu.VMEM((4, 6, 8, Z), F32),
            pltpu.VMEM((n * rows, slots), F32),
            pltpu.VMEM((n * rows, slots), F32),
            pltpu.VMEM((n * back_rows, slots), F32),
            pltpu.VMEM((n * back_rows, slots), F32),
            pltpu.SemaphoreType.DMA((n,)),
            pltpu.SemaphoreType.DMA((n,)),
            pltpu.SemaphoreType.DMA((4,)),
            pltpu.SemaphoreType.DMA((4,)),
            pltpu.SemaphoreType.DMA((4,)),
            pltpu.SemaphoreType.DMA((4,)),
            pltpu.SemaphoreType.DMA((n,)),
            pltpu.SemaphoreType.DMA((n,)),
        ],
        compiler_params=pltpu.CompilerParams(
            collective_id=0, has_side_effects=True, vmem_limit_bytes=32 * 1024 * 1024
        ),
    )(*(pltpu.with_memory_space_constraint(x, pltpu.HBM) for x in operands))
    hbm = pl.BlockSpec(memory_space=pltpu.HBM)
    fields, velocity = pl.pallas_call(
        put_out,
        out_shape=(
            jax.ShapeDtypeStruct((4, X * Y, Z), F32),
            jax.ShapeDtypeStruct((3, blocks, slots), F32),
        ),
        in_specs=[vmem, vmem],
        out_specs=(hbm, hbm),
        scratch_shapes=[pltpu.SemaphoreType.DMA((2,))],
        compiler_params=pltpu.CompilerParams(vmem_limit_bytes=32 * 1024 * 1024),
    )(fields, velocity)
    return fields.reshape(4, X, Y, Z), velocity


def solution(mesh):
    return jax.shard_map(
        shards,
        mesh=mesh,
        in_specs=(
            P(None, "gx", "yz", None),
            P("gx", "yz", None),
            P(None, ("gx", "yz"), None),
            P(("gx", "yz"), None),
            P(None, None, ("gx", "yz"), None),
            P(("gx", "yz"), None),
            P(("gx", "yz")),
            P(("gx", "yz")),
            P(("gx", "yz")),
            P(("gx", "yz"), None),
            P(("gx", "yz")),
        ),
        out_specs=(P(None, "gx", "yz", None), P(None, ("gx", "yz"), None)),
        check_vma=False,
    )
```
